256 devices in a mesh: grp: 4 (over x_lo, core), cl: 64 (over x_hi, y, z).
Axes of the slice: x: 4 (x_hi: 2, x_lo: 2; x = x_hi * 2 + x_lo), y: 4, z: 8, core: 2. Of those that a mesh axis runs over, the one named last changes fastest.
Arguments:
- incident: float32 [128, 128, 512], P('cl', None, 'grp'), may hold values from -6 to 6
- near_real: float32 [128, 16, 128, 128], P('cl'), may hold values from -0.0625 to 0.0625
- near_imag: float32 [128, 16, 128, 128], P('cl'), may hold values from -0.0625 to 0.0625
- to_moments: float32 [128, 128, 128], P('cl'), may hold values from -0.5 to 0.5
- from_locals: float32 [128, 128, 128], P('cl'), may hold values from -0.25 to 0.25
- transfer_ops: float32 [16, 128, 128], replicated, may hold values from -0.09375 to 0.09375
- near_index: int32 [128, 16], P('cl'), may hold values from 0 to 5
- near_count: int32 [128], P('cl'), may hold values from 1 to 16
- cluster_box: int32 [128], P('cl'), may hold values from 0 to 1
- far_source: int32 [128, 32], P('cl'), may hold values from 0 to 127
- far_kind: int32 [128, 32], P('cl'), may hold values from 0 to 15
- far_count: int32 [128], P('cl'), may hold values from 8 to 32
Outputs:
- pressure: float32 [128, 128, 512], P('cl', None, 'grp')
- residual: float32 [128, 128, 512], P('cl', None, 'grp')
The draws below stay inside these ranges and needn't reach their ends.
Inputs may be any that keep to these rules, and one draw needn't show every extreme that they name: `near_index`: positions 0 to 1 are the clusters of the previous slab along cl (wrapping), then this slab's, then the next slab's. `far_source`: global box numbers.
All inputs are finite; a program needn't handle non-finite values.
Results may differ from the reference program's by a relative error of at most 0.0003.
Values sent between devices are 32-bit elements; how exact they have to be, the bound alone decides.
No kernel may reach another device: no remote copies, remote signals or barrier semaphores. Data moves between devices by JAX's collectives and lax.ppermute only.
A program may use at most 64 MiB of HBM per device.

```python
import jax
import jax.numpy as jnp
from jax import lax

DIRS = 512
POINTS = 128
COEFFS = 128
CL_DEV = 2
BOX_DEV = 2
NEAR_MAX = 16
FAR_MAX = 32
KINDS = 16
ITERS = 2
CLUSTERS = 128
BOXES = 128
N_CL = 64


def set_ends(values, own_key, smallest, high):
    index_at = [jax.random.randint(jax.random.fold_in(own_key, axis), (), 0, length) for axis, length in enumerate(values.shape)]
    longest = values.shape.index(max(values.shape))
    neighbour = index_at[:longest] + [(index_at[longest] + 1) % values.shape[longest]] + index_at[longest + 1:]
    return values.at[tuple(index_at)].set(smallest).at[tuple(neighbour)].set(high)


def level_of(stream_key, dims, split, low, high):
    factor_of = 1.0
    for position, parts in split:
        draws = jax.random.uniform(jax.random.fold_in(jax.random.fold_in(stream_key, 6), position), (parts,), jnp.float32, low / len(split), high / len(split))
        factor_of = factor_of * jnp.repeat(jnp.exp(draws), dims[position] // parts).reshape((-1,) + (1,) * (len(dims) - 1 - position))
    return factor_of


def centred(own_key, extent, spread, limit, split=(), kind=jnp.bfloat16):
    entries = jax.random.normal(own_key, extent, jnp.float32) * spread
    if len(split) > 0:
        entries = level_of(own_key, extent, split, -0.22, 0.18) * entries
    return jnp.clip(entries, min=-limit, max=limit).astype(kind)


def setup_inputs(seed: int = 0) -> dict:
    arg_keys = jax.random.split(jax.random.key(seed), 13)
    incident = centred(arg_keys[0], (CLUSTERS, POINTS, DIRS), 1.0, 6.0, ((0, 64), (2, 4)), jnp.float32)
    near_real = centred(arg_keys[1], (CLUSTERS, NEAR_MAX, POINTS, POINTS), (4 * POINTS * NEAR_MAX) ** -0.5, 0.0625, ((0, 64),), jnp.float32)
    near_imag = centred(arg_keys[2], (CLUSTERS, NEAR_MAX, POINTS, POINTS), (4 * POINTS * NEAR_MAX) ** -0.5, 0.0625, ((0, 64),), jnp.float32)
    to_moments = centred(arg_keys[3], (CLUSTERS, COEFFS, POINTS), POINTS ** -0.5, 0.5, ((0, 64),), jnp.float32)
    from_locals = centred(arg_keys[4], (CLUSTERS, POINTS, COEFFS), (4 * COEFFS) ** -0.5, 0.25, ((0, 64),), jnp.float32)
    transfer_ops = centred(arg_keys[5], (KINDS, COEFFS, COEFFS), (COEFFS * FAR_MAX) ** -0.5, 0.09375, (), jnp.float32)
    near_index = set_ends(jax.random.randint(arg_keys[6], (CLUSTERS, NEAR_MAX), 0, 3 * CL_DEV), jax.random.fold_in(arg_keys[6], 1), 0, (3 * CL_DEV) - 1).astype(jnp.int32)
    near_count = set_ends(jax.random.randint(arg_keys[7], (CLUSTERS,), 1, NEAR_MAX + 1), jax.random.fold_in(arg_keys[7], 1), 1, NEAR_MAX).astype(jnp.int32)
    cluster_box = set_ends(jax.random.randint(arg_keys[8], (CLUSTERS,), 0, BOX_DEV), jax.random.fold_in(arg_keys[8], 1), 0, BOX_DEV - 1).astype(jnp.int32)
    far_source = set_ends(jax.random.randint(arg_keys[9], (BOXES, FAR_MAX), 0, BOXES), jax.random.fold_in(arg_keys[9], 1), 0, BOXES - 1).astype(jnp.int32)
    far_kind = set_ends(jax.random.randint(arg_keys[10], (BOXES, FAR_MAX), 0, KINDS), jax.random.fold_in(arg_keys[10], 1), 0, KINDS - 1).astype(jnp.int32)
    far_count = set_ends(jax.random.randint(arg_keys[11], (BOXES,), FAR_MAX // 4, FAR_MAX + 1), jax.random.fold_in(arg_keys[11], 1), FAR_MAX // 4, FAR_MAX).astype(jnp.int32)
    return dict(incident=incident, near_real=near_real, near_imag=near_imag, to_moments=to_moments, from_locals=from_locals, transfer_ops=transfer_ops, near_index=near_index, near_count=near_count, cluster_box=cluster_box, far_source=far_source, far_kind=far_kind, far_count=far_count)


DAMPING = 0.7


def operator_product(form, left, right):
    return jnp.einsum(form, left, right, precision=lax.Precision.HIGHEST)


def near_apply(iterate, near_real, near_imag, near_index, near_count):
    clusters, points, width = iterate.shape
    half = width // 2
    rotated_result = jnp.concatenate([-iterate[:, :, half:], iterate[:, :, :half]], axis=2)

    def one_block(inputs):
        block_index, real_blocks, imag_blocks, indices, counts = inputs
        sources = jnp.mod((block_index - 1) * CL_DEV + indices, clusters).astype(jnp.int32)
        live = (jnp.arange(NEAR_MAX, dtype=jnp.int32)[None, :] < counts[:, None]).astype(iterate.dtype)
        plain = jnp.take(iterate, sources, axis=0) * live[:, :, None, None]
        crossed = jnp.take(rotated_result, sources, axis=0) * live[:, :, None, None]
        return operator_product("cepq,ceqk->cpk", real_blocks, plain) + operator_product("cepq,ceqk->cpk", imag_blocks, crossed)

    inputs = (jnp.arange(N_CL, dtype=jnp.int32),
              near_real.reshape(N_CL, CL_DEV, NEAR_MAX, points, points),
              near_imag.reshape(N_CL, CL_DEV, NEAR_MAX, points, points),
              near_index.reshape(N_CL, CL_DEV, NEAR_MAX),
              near_count.reshape(N_CL, CL_DEV))
    return lax.map(one_block, inputs).reshape(clusters, points, width)


def far_apply(iterate, to_moments, from_locals, transfer_ops, cluster_box, far_source, far_kind, far_count):
    owner = ((jnp.arange(CLUSTERS, dtype=jnp.int32) // CL_DEV) * BOX_DEV + cluster_box).astype(jnp.int32)
    multipole_series = operator_product("cqp,cpk->cqk", to_moments, iterate)
    moment_values = jax.ops.segment_sum(multipole_series, owner, num_segments=BOXES)

    def one_target(inputs):
        sources, kinds, counts = inputs
        live = (jnp.arange(FAR_MAX, dtype=jnp.int32) < counts).astype(iterate.dtype)
        operators = jnp.take(transfer_ops, kinds, axis=0) * live[:, None, None]
        return operator_product("frq,fqk->rk", operators, jnp.take(moment_values, sources, axis=0))

    local_field = lax.map(one_target, (far_source, far_kind, far_count))
    return operator_product("cpr,crk->cpk", from_locals, jnp.take(local_field, owner, axis=0))


def reference(incident, near_real, near_imag, to_moments, from_locals, transfer_ops, near_index, near_count, cluster_box, far_source, far_kind, far_count):
    pressure = incident
    residual = jnp.zeros_like(incident)
    for iteration in range(ITERS):
        applied = pressure + near_apply(pressure, near_real, near_imag, near_index, near_count)
        applied = applied + far_apply(pressure, to_moments, from_locals, transfer_ops, cluster_box, far_source, far_kind, far_count)
        residual = incident - applied
        pressure = pressure + DAMPING * residual
    return pressure, residual
```

```python
import functools

import jax
import jax.numpy as jnp
from jax import lax
from jax.experimental import pallas as pl
from jax.experimental.pallas import tpu as pltpu
from jax.sharding import PartitionSpec as P

ITERS = 2
DAMPING = 0.7
F32, BF16 = jnp.float32, jnp.bfloat16
VMEM = pl.BlockSpec(memory_space=pltpu.VMEM)
SMEM = pl.BlockSpec(memory_space=pltpu.SMEM)
NT = (((1,), (1,)), ((), ()))
NN = (((1,), (0,)), ((), ()))


def halves(x):
    top = x.astype(BF16)
    return top, (x - top.astype(F32)).astype(BF16)


def dot(a, b, dims=NN):
    return lax.dot_general(a, b, dims, preferred_element_type=F32)


def product(a, b, dims=NN):
    (a0, a1), (b0, b1) = halves(a), halves(b)
    return dot(a0, b0, dims) + (dot(a0, b1, dims) + dot(a1, b0, dims))


def call(body, outs, in_specs, out_specs, name, mib=16, cycles=0, **more):
    return pl.pallas_call(
        body,
        out_shape=outs,
        in_specs=in_specs,
        out_specs=out_specs,
        name=name,
        compiler_params=pltpu.CompilerParams(vmem_limit_bytes=mib << 20),
        cost_estimate=pl.CostEstimate(flops=cycles, bytes_accessed=1 << 18, transcendentals=0),
        **more,
    )


def send_moments(field, to_moments_ref, box_ref, out_ref, rows):
    count, peers = len(field), out_ref.shape[0] // rows
    series = [product(to_moments_ref[c], field[c]).T for c in range(count)]
    for b in range(count):
        moment = sum(jnp.where(box_ref[c] == b, series[c], 0.0) for c in range(count))
        for k in range(2):
            out_ref[pl.ds(2 * b + k, peers, stride=rows), :] = moment[k * peers : (k + 1) * peers]


def first_moments_body(rows, field_ref, to_moments_ref, source_ref, kind_ref, count_ref, box_ref, out_ref):
    boxes, most = source_ref.shape
    peers = out_ref.shape[0] // rows
    at = lax.broadcasted_iota(jnp.int32, (1, most), 1)
    kinds = [jnp.where(at < count_ref[b], kind_ref[b : b + 1, :], -1) for b in range(boxes)]
    lists = jnp.concatenate([source_ref[b : b + 1, :] for b in range(boxes)] + kinds, axis=1).astype(F32)
    send_moments([field_ref[0], field_ref[1]], to_moments_ref, box_ref, out_ref, rows)
    out_ref[pl.ds(4, peers, stride=rows), :] = jnp.broadcast_to(lists, (peers, lists.shape[1]))
    for row in range(5, rows):
        out_ref[pl.ds(row, peers, stride=rows), :] = jnp.zeros((peers, lists.shape[1]), F32)


def blocks_body(index_ref, count_ref, sign_ref, real_ref, imag_ref, top_ref, rest_ref, total):
    c, part = pl.program_id(0), pl.program_id(1)
    chunk = real_ref.shape[1]

    @pl.when((c == 0) & (part == 0))
    def _():
        total[...] = jnp.zeros_like(total)

    for i in range(chunk):
        e = part * chunk + i

        @pl.when(e < count_ref[c])
        def _():
            j = index_ref[c, e]
            total[j, c, 0] += real_ref[0, i]
            total[j, c, 1] += imag_ref[0, i]

    @pl.when((c == pl.num_programs(0) - 1) & (part == pl.num_programs(1) - 1))
    def _():
        points = total.shape[3]
        for j in range(total.shape[0]):
            for cluster in range(total.shape[1]):
                for side in range(2):
                    block = total[j, cluster, side]
                    if side == 1:
                        block = block * sign_ref[0]
                    top, rest = halves(block)
                    row = (cluster * 2 + side) * points
                    here = (j // 2, pl.ds(row, points), pl.ds(j % 2 * points, points))
                    top_ref[here] = top
                    rest_ref[here] = rest


def operators_body(ops_ref, out_ref):
    size = ops_ref.shape[1]
    for y in range(ops_ref.shape[0]):
        top, rest = halves(ops_ref[y].T)
        rows = pl.ds(y % 2 * size, size)
        out_ref[y // 2, rows, 0:size] = top
        out_ref[y // 2, rows, size : 2 * size] = rest


def near_body(before_ref, own_ref, after_ref, top_ref, rest_ref, straight_ref, crossed_ref):
    points = own_ref.shape[1]
    total = None
    for slab, ref in enumerate((before_ref, own_ref, after_ref)):
        v0, v1 = halves(jnp.concatenate([ref[0], ref[1]], axis=0))
        both = dot(top_ref[slab], jnp.concatenate([v0, v1], axis=1))
        part = both[:, :points] + (both[:, points:] + dot(rest_ref[slab], v0))
        total = part if total is None else total + part
    for c in range(2):
        straight_ref[c] = total[2 * c * points : (2 * c + 1) * points]
        crossed_ref[c] = total[(2 * c + 1) * points : (2 * c + 2) * points]


def interaction_counts(in_ref, rows, counts_ref, kinds):
    peers = in_ref.shape[0] // rows
    parts = [in_ref[pl.ds(4 + rows * j, peers // 4, stride=4 * rows), :] for j in range(4)]
    lane = lax.broadcasted_iota(jnp.int32, parts[0].shape, 1)
    low = lane < 64
    turn = [pltpu.roll(p, 64, 1) for p in parts]
    source = jnp.concatenate([jnp.where(low, parts[0], turn[1]), jnp.where(low, parts[2], turn[3])], axis=1)
    kind = jnp.concatenate([jnp.where(low, turn[0], parts[1]), jnp.where(low, turn[2], parts[3])], axis=1)
    source, kind = source.astype(jnp.int32), kind.astype(jnp.int32)
    source = (source & 1) * peers + (source >> 1)
    wide = source.shape[1]
    row = lax.broadcasted_iota(jnp.int32, (2 * peers, wide), 0)
    column = lax.broadcasted_iota(jnp.int32, (2 * peers, wide), 1)
    own = (row & 7) == (column >> 5)
    for i in range(peers // 4):
        left = jnp.where(own & ((row >> 3) == kind[i : i + 1, :]), 1.0, 0.0).astype(BF16)
        right = jnp.where(row == source[i : i + 1, :], 1.0, 0.0).astype(BF16)
        block = dot(left, right, NT).astype(BF16)
        for y in range(kinds):
            counts_ref[y, 8 * i : 8 * i + 8, :] = block[8 * y : 8 * y + 8]


def transfer(in_ref, rows, ops_ref, counts_ref, out_ref):
    peers, size = in_ref.shape[0] // rows, in_ref.shape[1]
    moments = []
    for k in range(2):
        moments.append(
            jnp.concatenate([in_ref[pl.ds(2 * b + k, peers, stride=rows), :] for b in range(2)], axis=0)
        )
    m0, m1 = halves(jnp.concatenate(moments, axis=1))
    right = jnp.concatenate([m0, m1], axis=0)
    total = [None, None]
    for pair in range(ops_ref.shape[0]):
        grouped = []
        for y in (2 * pair, 2 * pair + 1):
            count = counts_ref[y]
            grouped.append(dot(jnp.concatenate([count, count], axis=1), right))
        for k in range(2):
            g0, g1 = halves(jnp.concatenate([g[:, k * size : (k + 1) * size] for g in grouped], axis=1))
            both = dot(g0, ops_ref[pair])
            part = both[:, :size] + (both[:, size:] + dot(g1, ops_ref[pair, :, :size]))
            total[k] = part if total[k] is None else total[k] + part
    for k in range(2):
        out_ref[pl.ds(k, 2 * peers, stride=2), :] = total[k]


def first_transfer_body(rows, in_ref, ops_ref, out_ref, counts_ref):
    interaction_counts(in_ref, rows, counts_ref, counts_ref.shape[0])
    transfer(in_ref, rows, ops_ref, counts_ref, out_ref)


def next_transfer_body(rows, in_ref, ops_ref, counts_ref, out_ref):
    transfer(in_ref, rows, ops_ref, counts_ref, out_ref)


def update_body(last, in_ref, from_locals_ref, to_moments_ref, box_ref, straight_ref, crossed_ref, incident_ref, pressure_ref, *outs):
    peers = in_ref.shape[0] // 4
    local = []
    for b in range(2):
        local.append(jnp.concatenate([in_ref[pl.ds(2 * b + k, peers, stride=4), :] for k in range(2)], axis=0))
    fields = []
    for c in range(2):
        far = product(from_locals_ref[c], jnp.where(box_ref[c] == 0, local[0], local[1]), NT)
        applied = pressure_ref[c] + (straight_ref[c] + crossed_ref[c]) + far
        residual = incident_ref[c] - applied
        field = pressure_ref[c] + DAMPING * residual
        fields.append(field)
        outs[0][c] = field
        if last:
            outs[1][c] = residual
    if not last:
        send_moments(fields, to_moments_ref, box_ref, outs[1], 4)


def shards(
    incident,
    near_real,
    near_imag,
    to_moments,
    from_locals,
    transfer_ops,
    near_index,
    near_count,
    cluster_box,
    far_source,
    far_kind,
    far_count,
):
    clusters, points, width = incident.shape
    near_max = near_real.shape[1]
    peers, grp = lax.axis_size("cl"), lax.axis_size("grp")
    kinds, size = transfer_ops.shape[0], transfer_ops.shape[1]
    field = jax.ShapeDtypeStruct(incident.shape, F32)
    rows = 8
    forward = [(i, (i + 1) % peers) for i in range(peers)]
    backward = [(target, source) for source, target in forward]
    across = [(i, (i + grp // 2) % grp) for i in range(grp)]
    sign = jnp.where(lax.axis_index("grp") < grp // 2, 1.0, -1.0).astype(F32).reshape(1)

    def exchange(x, pieces):
        x = x.reshape(peers, pieces, size)
        return lax.all_to_all(x, "cl", split_axis=0, concat_axis=0, tiled=True).reshape(-1, size)

    chunk = 4
    block = pl.BlockSpec((1, chunk, points, points), lambda c, part: (c, part, 0, 0))
    halved = jax.ShapeDtypeStruct((3, 4 * points, 2 * points), BF16)
    whole = pl.BlockSpec(halved.shape, lambda c, part: (0, 0, 0))
    blocks_top, blocks_rest = call(
        blocks_body,
        (halved, halved),
        [SMEM, SMEM, SMEM, block, block],
        (whole, whole),
        "neighbour_blocks",
        grid=(clusters, near_max // chunk),
        scratch_shapes=[pltpu.VMEM((6, clusters, 2, points, points), F32)],
    )(near_index, near_count, sign, near_real, near_imag)
    operators = call(
        operators_body,
        jax.ShapeDtypeStruct((kinds // 2, 2 * size, 2 * size), BF16),
        [VMEM],
        VMEM,
        "operators",
    )(transfer_ops)
    sent = call(
        functools.partial(first_moments_body, rows),
        jax.ShapeDtypeStruct((peers * rows, size), F32),
        [VMEM] * 4 + [SMEM] * 2,
        VMEM,
        "first_moments",
    )(incident, to_moments, far_source, far_kind, far_count, cluster_box)

    pressure = incident
    for iteration in range(ITERS):
        first, last = iteration == 0, iteration == ITERS - 1
        before = lax.ppermute(pressure, "cl", forward)
        after = lax.ppermute(pressure, "cl", backward)
        arrived = exchange(sent, rows if first else 4)
        straight, crossed = call(near_body, (field, field), [VMEM] * 5, (VMEM, VMEM), "near")(
            before, pressure, after, blocks_top, blocks_rest
        )
        crossed = lax.ppermute(crossed, "grp", across)
        piece = jax.ShapeDtypeStruct((peers * 4, size), F32)
        if first:
            locals_out, counts = call(
                functools.partial(first_transfer_body, rows),
                (piece, jax.ShapeDtypeStruct((kinds, 2 * peers, 2 * peers), BF16)),
                [VMEM] * 2,
                (VMEM, VMEM),
                "first_transfer",
            )(arrived, operators)
        else:
            locals_out = call(
                functools.partial(next_transfer_body, 4), piece, [VMEM] * 3, VMEM, "next_transfer"
            )(arrived, operators, counts)
        local = exchange(locals_out, 4)
        pressure, sent = call(
            functools.partial(update_body, last),
            (field, field if last else piece),
            [VMEM] * 3 + [SMEM] + [VMEM] * 4,
            (VMEM, VMEM),
            "update",
        )(local, from_locals, to_moments, cluster_box, straight, crossed, incident, pressure)
    return (pressure, sent)


def solution(mesh):
    return jax.shard_map(
        shards,
        mesh=mesh,
        in_specs=(
            P("cl", None, "grp"),
            P("cl", None, None, None),
            P("cl", None, None, None),
            P("cl", None, None),
            P("cl", None, None),
            P(),
            P("cl", None),
            P("cl"),
            P("cl"),
            P("cl", None),
            P("cl", None),
            P("cl"),
        ),
        out_specs=(P("cl", None, "grp"), P("cl", None, "grp")),
        check_vma=False,
    )
```

```python
import functools

import jax
import jax.numpy as jnp
from jax import lax
from jax.experimental import pallas as pl
from jax.experimental.pallas import tpu as pltpu
from jax.sharding import PartitionSpec as P


ITERS = 2
DAMPING = 0.7
MIB = (8, 8, 8)
F32, BF16 = jnp.float32, jnp.bfloat16
VMEM = pl.BlockSpec(memory_space=pltpu.VMEM)
SMEM = pl.BlockSpec(memory_space=pltpu.SMEM)
NT = (((1,), (1,)), ((), ()))
NN = (((1,), (0,)), ((), ()))


def halves(x):
    top = x.astype(BF16)
    return top, (x - top.astype(F32)).astype(BF16)


def dot(a, b, dims=NN):
    return lax.dot_general(a, b, dims, preferred_element_type=F32)


def product(a, b, dims=NN):
    (a0, a1), (b0, b1) = halves(a), halves(b)
    return dot(a0, b0, dims) + (dot(a0, b1, dims) + dot(a1, b0, dims))


def call(body, outs, in_specs, out_specs, mib=8, cycles=0, **more):
    return pl.pallas_call(
        body,
        out_shape=outs,
        in_specs=in_specs,
        out_specs=out_specs,
        compiler_params=pltpu.CompilerParams(vmem_limit_bytes=mib << 20),
        cost_estimate=pl.CostEstimate(flops=cycles, bytes_accessed=1 << 18, transcendentals=0),
        **more,
    )


def send_moments(field, to_moments_ref, box_ref, out_ref, rows):
    count, peers = len(field), out_ref.shape[0] // rows
    series = [product(to_moments_ref[c], field[c]).T for c in range(count)]
    for b in range(count):
        moment = sum(jnp.where(box_ref[c] == b, series[c], 0.0) for c in range(count))
        for k in range(2):
            out_ref[pl.ds(2 * b + k, peers, stride=rows), :] = moment[k * peers : (k + 1) * peers]


def first_moments_body(rows, field_ref, to_moments_ref, source_ref, kind_ref, count_ref, box_ref, out_ref):
    boxes, most = source_ref.shape
    peers = out_ref.shape[0] // rows
    at = lax.broadcasted_iota(jnp.int32, (1, most), 1)
    kinds = [jnp.where(at < count_ref[b], kind_ref[b : b + 1, :], -1) for b in range(boxes)]
    lists = jnp.concatenate([source_ref[b : b + 1, :] for b in range(boxes)] + kinds, axis=1).astype(F32)
    send_moments([field_ref[0], field_ref[1]], to_moments_ref, box_ref, out_ref, rows)
    out_ref[pl.ds(4, peers, stride=rows), :] = jnp.broadcast_to(lists, (peers, lists.shape[1]))
    for row in range(5, rows):
        out_ref[pl.ds(row, peers, stride=rows), :] = jnp.zeros((peers, lists.shape[1]), F32)


def blocks_body(index_ref, count_ref, place_ref, sign_ref, real_ref, imag_ref, top_ref, rest_ref, total):
    odd = lax.rem(place_ref[0], 2)
    c, part = pl.program_id(0), pl.program_id(1)
    chunk = real_ref.shape[1]

    @pl.when((c == 0) & (part == 0))
    def _():
        total[...] = jnp.zeros_like(total)

    for i in range(chunk):
        e = part * chunk + i

        @pl.when(e < count_ref[c])
        def _():
            j = index_ref[c, e]
            total[j, c, 0] += real_ref[0, i]
            total[j, c, 1] += imag_ref[0, i]

    @pl.when((c == pl.num_programs(0) - 1) & (part == pl.num_programs(1) - 1))
    def _():
        points = total.shape[3]
        for j in range(total.shape[0]):
            for cluster in range(total.shape[1]):
                for side in range(2):
                    block = total[j, cluster, side]
                    if side == 1:
                        block = block * sign_ref[0]
                    top, rest = halves(block)
                    row = (cluster * 2 + side) * points
                    slot = (2 - 2 * odd, 1, 2 * odd)[j // 2]
                    here = (slot, pl.ds(row, points), pl.ds(j % 2 * points, points))
                    top_ref[here] = top
                    rest_ref[here] = rest


def operators_body(ops_ref, out_ref):
    size = ops_ref.shape[1]
    for y in range(ops_ref.shape[0]):
        top, rest = halves(ops_ref[y].T)
        rows = pl.ds(y % 2 * size, size)
        out_ref[y // 2, rows, 0:size] = top
        out_ref[y // 2, rows, size : 2 * size] = rest


def near_body(first_ref, own_ref, second_ref, top_ref, rest_ref, straight_ref, crossed_ref):
    points = own_ref.shape[1]
    total = None
    for slot, ref in enumerate((first_ref, own_ref, second_ref)):
        v0, v1 = halves(jnp.concatenate([ref[0], ref[1]], axis=0))
        both = dot(top_ref[slot], jnp.concatenate([v0, v1], axis=1))
        part = both[:, :points] + (both[:, points:] + dot(rest_ref[slot], v0))
        total = part if total is None else total + part
    for c in range(2):
        straight_ref[c] = total[2 * c * points : (2 * c + 1) * points]
        crossed_ref[c] = total[(2 * c + 1) * points : (2 * c + 2) * points]


def interaction_counts(lists_ref, first, step, peers, counts_ref):
    parts = [lists_ref[pl.ds(first + step * j, peers // 4, stride=4 * step), :] for j in range(4)]
    lane = lax.broadcasted_iota(jnp.int32, parts[0].shape, 1)
    low = lane < 64
    turn = [pltpu.roll(p, 64, 1) for p in parts]
    source = jnp.concatenate([jnp.where(low, parts[0], turn[1]), jnp.where(low, parts[2], turn[3])], axis=1)
    kind = jnp.concatenate([jnp.where(low, turn[0], parts[1]), jnp.where(low, turn[2], parts[3])], axis=1)
    source, kind = source.astype(jnp.int32), kind.astype(jnp.int32)
    source = (source & 1) * peers + (source >> 1)
    wide = source.shape[1]
    row = lax.broadcasted_iota(jnp.int32, (2 * peers, wide), 0)
    column = lax.broadcasted_iota(jnp.int32, (2 * peers, wide), 1)
    own = (row & 7) == (column >> 5)
    for i in range(peers // 4):
        left = jnp.where(own & ((row >> 3) == kind[i : i + 1, :]), 1.0, 0.0).astype(BF16)
        right = jnp.where(row == source[i : i + 1, :], 1.0, 0.0).astype(BF16)
        block = dot(left, right, NT).astype(BF16)
        for y in range(counts_ref.shape[0]):
            counts_ref[y, 8 * i : 8 * i + 8, :] = block[8 * y : 8 * y + 8]


def transfer(in_ref, rows, ops_ref, counts_ref, out_ref):
    peers, size = in_ref.shape[0] // rows, in_ref.shape[1]
    moments = []
    for k in range(2):
        moments.append(
            jnp.concatenate([in_ref[pl.ds(2 * b + k, peers, stride=rows), :] for b in range(2)], axis=0)
        )
    m0, m1 = halves(jnp.concatenate(moments, axis=1))
    right = jnp.concatenate([m0, m1], axis=0)
    total = [None, None]
    for pair in range(ops_ref.shape[0]):
        grouped = []
        for y in (2 * pair, 2 * pair + 1):
            count = counts_ref[y]
            grouped.append(dot(jnp.concatenate([count, count], axis=1), right))
        for k in range(2):
            g0, g1 = halves(jnp.concatenate([g[:, k * size : (k + 1) * size] for g in grouped], axis=1))
            both = dot(g0, ops_ref[pair])
            part = both[:, :size] + (both[:, size:] + dot(g1, ops_ref[pair, :, :size]))
            total[k] = part if total[k] is None else total[k] + part
    for k in range(2):
        out_ref[pl.ds(k, 2 * peers, stride=2), :] = total[k]


def first_transfer_body(rows, in_ref, ops_ref, out_ref, lists_ref, counts_ref):
    peers = in_ref.shape[0] // rows
    lists_ref[...] = in_ref[pl.ds(4, peers, stride=rows), :]
    interaction_counts(in_ref, 4, rows, peers, counts_ref)
    transfer(in_ref, rows, ops_ref, counts_ref, out_ref)


def next_transfer_body(in_ref, ops_ref, lists_ref, out_ref, counts_ref):
    interaction_counts(lists_ref, 0, 1, lists_ref.shape[0], counts_ref)
    transfer(in_ref, 4, ops_ref, counts_ref, out_ref)


def update_body(last, in_ref, from_locals_ref, to_moments_ref, box_ref, straight_ref, crossed_ref, incident_ref, pressure_ref, *outs):
    peers = in_ref.shape[0] // 4
    local = []
    for b in range(2):
        local.append(jnp.concatenate([in_ref[pl.ds(2 * b + k, peers, stride=4), :] for k in range(2)], axis=0))
    fields = []
    for c in range(2):
        far = product(from_locals_ref[c], jnp.where(box_ref[c] == 0, local[0], local[1]), NT)
        applied = pressure_ref[c] + (straight_ref[c] + crossed_ref[c]) + far
        residual = incident_ref[c] - applied
        field = pressure_ref[c] + DAMPING * residual
        fields.append(field)
        outs[0][c] = field
        if last:
            outs[1][c] = residual
    if not last:
        send_moments(fields, to_moments_ref, box_ref, outs[1], 4)


def shards(
    incident,
    near_real,
    near_imag,
    to_moments,
    from_locals,
    transfer_ops,
    near_index,
    near_count,
    cluster_box,
    far_source,
    far_kind,
    far_count,
):
    clusters, points, _ = incident.shape
    near_max = near_real.shape[1]
    peers, grp = lax.axis_size("cl"), lax.axis_size("grp")
    kinds, size = transfer_ops.shape[0], transfer_ops.shape[1]
    field = jax.ShapeDtypeStruct(incident.shape, F32)
    rows = 8
    first_swap = [(i, i ^ 1) for i in range(peers)]
    second_swap = [(i, (i + 1 if i % 2 else i - 1) % peers) for i in range(peers)]
    across = [(i, (i + grp // 2) % grp) for i in range(grp)]
    sign = jnp.where(lax.axis_index("grp") < grp // 2, 1.0, -1.0).astype(F32).reshape(1)

    place = lax.axis_index("cl").astype(jnp.int32).reshape(1)

    def exchange(x, pieces):
        x = x.reshape(peers, pieces, size)
        return lax.all_to_all(x, "cl", split_axis=0, concat_axis=0, tiled=True).reshape(-1, size)

    chunk = 8
    block = pl.BlockSpec((1, chunk, points, points), lambda c, part: (c, part, 0, 0))
    halved = jax.ShapeDtypeStruct((3, 2 * clusters * points, 2 * points), BF16)
    whole = pl.BlockSpec(halved.shape, lambda c, part: (0, 0, 0))
    blocks = call(
        blocks_body,
        (halved, halved),
        [SMEM] * 4 + [block] * 2,
        (whole, whole),
        mib=56,
        grid=(clusters, near_max // chunk),
        scratch_shapes=[pltpu.VMEM((6, clusters, 2, points, points), F32)],
    )
    prepare = call(operators_body, jax.ShapeDtypeStruct((kinds // 2, 2 * size, 2 * size), BF16), [VMEM], VMEM)
    sent = call(
        functools.partial(first_moments_body, rows),
        jax.ShapeDtypeStruct((peers * rows, size), F32),
        [VMEM] * 4 + [SMEM] * 2,
        VMEM,
        mib=56,
    )(incident, to_moments, far_source, far_kind, far_count, cluster_box)

    pressure = incident
    for iteration in range(ITERS):
        first, last = iteration == 0, iteration == ITERS - 1
        arrived = exchange(sent, rows if first else 4)
        if first:
            blocks_top, blocks_rest = blocks(near_index, near_count, place, sign, near_real, near_imag)
            operators = prepare(transfer_ops)
        one = lax.ppermute(pressure, "cl", first_swap)
        two = lax.ppermute(pressure, "cl", second_swap)
        piece = jax.ShapeDtypeStruct((peers * 4, size), F32)
        scratch = [pltpu.VMEM((kinds, 2 * peers, 2 * peers), BF16)]
        if first:
            locals_out, lists = call(
                functools.partial(first_transfer_body, rows),
                (piece, jax.ShapeDtypeStruct((peers, size), F32)),
                [VMEM] * 2,
                (VMEM, VMEM),
                scratch_shapes=scratch,
                mib=MIB[1],
            )(arrived, operators)
        else:
            locals_out = call(
                next_transfer_body, piece, [VMEM] * 3, VMEM, scratch_shapes=scratch, mib=MIB[1]
            )(arrived, operators, lists)
        local = exchange(locals_out, 4)
        straight, crossed = call(
            near_body, (field, field), [VMEM] * 5, (VMEM, VMEM), mib=MIB[0]
        )(one, pressure, two, blocks_top, blocks_rest)
        crossed = lax.ppermute(crossed, "grp", across)
        pressure, sent = call(
            functools.partial(update_body, last),
            (field, field if last else piece),
            [VMEM] * 3 + [SMEM] + [VMEM] * 4,
            (VMEM, VMEM),
            mib=MIB[2],
        )(local, from_locals, to_moments, cluster_box, straight, crossed, incident, pressure)
    return (pressure, sent)


def solution(mesh):
    return jax.shard_map(
        shards,
        mesh=mesh,
        in_specs=(
            P("cl", None, "grp"),
            P("cl", None, None, None),
            P("cl", None, None, None),
            P("cl", None, None),
            P("cl", None, None),
            P(),
            P("cl", None),
            P("cl"),
            P("cl"),
            P("cl", None),
            P("cl", None),
            P("cl"),
        ),
        out_specs=(P("cl", None, "grp"), P("cl", None, "grp")),
        check_vma=False,
    )
```

```python
import functools

import jax
import jax.numpy as jnp
from jax import lax
from jax.experimental import pallas as pl
from jax.experimental.pallas import tpu as pltpu
from jax.sharding import PartitionSpec as P


ITERS = 2
DAMPING = 0.7
MIB = (8, 8, 8)
F32, BF16 = jnp.float32, jnp.bfloat16
VMEM = pl.BlockSpec(memory_space=pltpu.VMEM)
SMEM = pl.BlockSpec(memory_space=pltpu.SMEM)
NT = (((1,), (1,)), ((), ()))
NN = (((1,), (0,)), ((), ()))


def halves(x):
    top = x.astype(BF16)
    return top, (x - top.astype(F32)).astype(BF16)


def dot(a, b, dims=NN):
    return lax.dot_general(a, b, dims, preferred_element_type=F32)


def product(a, b, dims=NN):
    (a0, a1), (b0, b1) = halves(a), halves(b)
    return dot(a0, b0, dims) + (dot(a0, b1, dims) + dot(a1, b0, dims))


def call(body, outs, in_specs, out_specs, mib=8, cycles=0, **more):
    return pl.pallas_call(
        body,
        out_shape=outs,
        in_specs=in_specs,
        out_specs=out_specs,
        compiler_params=pltpu.CompilerParams(vmem_limit_bytes=mib << 20),
        cost_estimate=pl.CostEstimate(flops=cycles, bytes_accessed=1 << 18, transcendentals=0),
        **more,
    )


def send_moments(field, to_moments_ref, box_ref, out_ref, rows):
    count, peers = len(field), out_ref.shape[0] // rows
    series = [product(to_moments_ref[c], field[c]).T for c in range(count)]
    for b in range(count):
        moment = sum(jnp.where(box_ref[c] == b, series[c], 0.0) for c in range(count))
        for k in range(2):
            out_ref[pl.ds(2 * b + k, peers, stride=rows), :] = moment[k * peers : (k + 1) * peers]


def first_moments_body(rows, field_ref, to_moments_ref, source_ref, kind_ref, count_ref, box_ref, out_ref):
    boxes, most = source_ref.shape
    peers = out_ref.shape[0] // rows
    at = lax.broadcasted_iota(jnp.int32, (1, most), 1)
    kinds = [jnp.where(at < count_ref[b], kind_ref[b : b + 1, :], -1) for b in range(boxes)]
    lists = jnp.concatenate([source_ref[b : b + 1, :] for b in range(boxes)] + kinds, axis=1).astype(F32)
    send_moments([field_ref[0], field_ref[1]], to_moments_ref, box_ref, out_ref, rows)
    out_ref[pl.ds(4, peers, stride=rows), :] = jnp.broadcast_to(lists, (peers, lists.shape[1]))
    for row in range(5, rows):
        out_ref[pl.ds(row, peers, stride=rows), :] = jnp.zeros((peers, lists.shape[1]), F32)


def blocks_body(index_ref, count_ref, place_ref, sign_ref, real_ref, imag_ref, top_ref, rest_ref, total):
    odd = lax.rem(place_ref[0], 2)
    c, part = pl.program_id(0), pl.program_id(1)
    chunk = real_ref.shape[1]

    @pl.when((c == 0) & (part == 0))
    def _():
        total[...] = jnp.zeros_like(total)

    for i in range(chunk):
        e = part * chunk + i

        @pl.when(e < count_ref[c])
        def _():
            j = index_ref[c, e]
            total[j, c, 0] += real_ref[0, i]
            total[j, c, 1] += imag_ref[0, i]

    @pl.when((c == pl.num_programs(0) - 1) & (part == pl.num_programs(1) - 1))
    def _():
        points = total.shape[3]
        for j in range(total.shape[0]):
            for cluster in range(total.shape[1]):
                for side in range(2):
                    block = total[j, cluster, side]
                    if side == 1:
                        block = block * sign_ref[0]
                    top, rest = halves(block)
                    row = (cluster * 2 + side) * points
                    slot = (2 - 2 * odd, 1, 2 * odd)[j // 2]
                    here = (slot, pl.ds(row, points), pl.ds(j % 2 * points, points))
                    top_ref[here] = top
                    rest_ref[here] = rest


def operators_body(ops_ref, out_ref):
    size = ops_ref.shape[1]
    for y in range(ops_ref.shape[0]):
        top, rest = halves(ops_ref[y].T)
        rows = pl.ds(y % 2 * size, size)
        out_ref[y // 2, rows, 0:size] = top
        out_ref[y // 2, rows, size : 2 * size] = rest


def near_body(first, first_ref, own_ref, second_ref, top_ref, rest_ref, *rest):
    incident_ref = own_ref if first else rest[0]
    base_ref, crossed_ref = rest[-2:]
    points = own_ref.shape[1]
    total = None
    for slot, ref in enumerate((first_ref, own_ref, second_ref)):
        v0, v1 = halves(jnp.concatenate([ref[0], ref[1]], axis=0))
        both = dot(top_ref[slot], jnp.concatenate([v0, v1], axis=1))
        part = both[:, :points] + (both[:, points:] + dot(rest_ref[slot], v0))
        total = part if total is None else total + part
    for c in range(2):
        base_ref[c] = (incident_ref[c] - own_ref[c]) - total[2 * c * points : (2 * c + 1) * points]
        crossed_ref[c] = total[(2 * c + 1) * points : (2 * c + 2) * points]


def interaction_counts(in_ref, at, rows, counts_ref):
    peers = in_ref.shape[0] // rows
    parts = [in_ref[pl.ds(at + rows * j, peers // 4, stride=4 * rows), :] for j in range(4)]
    lane = lax.broadcasted_iota(jnp.int32, parts[0].shape, 1)
    low = lane < 64
    turn = [pltpu.roll(p, 64, 1) for p in parts]
    source = jnp.concatenate([jnp.where(low, parts[0], turn[1]), jnp.where(low, parts[2], turn[3])], axis=1)
    kind = jnp.concatenate([jnp.where(low, turn[0], parts[1]), jnp.where(low, turn[2], parts[3])], axis=1)
    source, kind = source.astype(jnp.int32), kind.astype(jnp.int32)
    source = (source & 1) * peers + (source >> 1)
    wide = source.shape[1]
    row = lax.broadcasted_iota(jnp.int32, (2 * peers, wide), 0)
    column = lax.broadcasted_iota(jnp.int32, (2 * peers, wide), 1)
    own = (row & 7) == (column >> 5)
    for i in range(peers // 4):
        left = jnp.where(own & ((row >> 3) == kind[i : i + 1, :]), 1.0, 0.0).astype(BF16)
        right = jnp.where(row == source[i : i + 1, :], 1.0, 0.0).astype(BF16)
        block = dot(left, right, NT).astype(BF16)
        for y in range(counts_ref.shape[0]):
            counts_ref[y, 8 * i : 8 * i + 8, :] = block[8 * y : 8 * y + 8]


def transfer(in_ref, ops_ref, counts_ref, out_ref, rows):
    peers, size = in_ref.shape[0] // rows, in_ref.shape[1]
    moments = []
    for k in range(2):
        moments.append(
            jnp.concatenate([in_ref[pl.ds(2 * b + k, peers, stride=rows), :] for b in range(2)], axis=0)
        )
    m0, m1 = halves(jnp.concatenate(moments, axis=1))
    right = jnp.concatenate([m0, m1], axis=0)
    total = [None, None]
    for pair in range(ops_ref.shape[0]):
        grouped = []
        for y in (2 * pair, 2 * pair + 1):
            count = counts_ref[y]
            grouped.append(dot(jnp.concatenate([count, count], axis=1), right))
        for k in range(2):
            g0, g1 = halves(jnp.concatenate([g[:, k * size : (k + 1) * size] for g in grouped], axis=1))
            both = dot(g0, ops_ref[pair])
            part = both[:, :size] + (both[:, size:] + dot(g1, ops_ref[pair, :, :size]))
            total[k] = part if total[k] is None else total[k] + part
    for k in range(2):
        out_ref[pl.ds(k, 2 * peers, stride=2), :] = total[k]


def first_transfer_body(rows, in_ref, ops_ref, out_ref, lists_ref, counts_ref):
    lists_ref[...] = in_ref[pl.ds(4, lists_ref.shape[0], stride=rows), :]
    interaction_counts(in_ref, 4, rows, counts_ref)
    transfer(in_ref, ops_ref, counts_ref, out_ref, rows)


def next_transfer_body(in_ref, ops_ref, lists_ref, out_ref, counts_ref):
    interaction_counts(lists_ref, 0, 1, counts_ref)
    transfer(in_ref, ops_ref, counts_ref, out_ref, 4)


def update_body(last, in_ref, from_locals_ref, to_moments_ref, box_ref, base_ref, crossed_ref, pressure_ref, *outs):
    peers = in_ref.shape[0] // 4
    local = []
    for b in range(2):
        local.append(jnp.concatenate([in_ref[pl.ds(2 * b + k, peers, stride=4), :] for k in range(2)], axis=0))
    fields = []
    for c in range(2):
        far = product(from_locals_ref[c], jnp.where(box_ref[c] == 0, local[0], local[1]), NT)
        residual = base_ref[c] - (crossed_ref[c] + far)
        field = pressure_ref[c] + DAMPING * residual
        fields.append(field)
        outs[0][c] = field
        if last:
            outs[1][c] = residual
    if not last:
        send_moments(fields, to_moments_ref, box_ref, outs[1], 4)


def shards(
    incident,
    near_real,
    near_imag,
    to_moments,
    from_locals,
    transfer_ops,
    near_index,
    near_count,
    cluster_box,
    far_source,
    far_kind,
    far_count,
):
    clusters, points, _ = incident.shape
    near_max = near_real.shape[1]
    peers, grp = lax.axis_size("cl"), lax.axis_size("grp")
    kinds, size = transfer_ops.shape[0], transfer_ops.shape[1]
    field = jax.ShapeDtypeStruct(incident.shape, F32)
    rows = 5
    first_swap = [(i, i ^ 1) for i in range(peers)]
    second_swap = [(i, (i + 1 if i % 2 else i - 1) % peers) for i in range(peers)]
    across = [(i, (i + grp // 2) % grp) for i in range(grp)]
    sign = jnp.where(lax.axis_index("grp") < grp // 2, 1.0, -1.0).astype(F32).reshape(1)

    place = lax.axis_index("cl").astype(jnp.int32).reshape(1)

    def exchange(x, pieces):
        x = x.reshape((peers, pieces, size) if pieces == 4 else (peers, pieces, 1, size))
        return lax.all_to_all(x, "cl", split_axis=0, concat_axis=0, tiled=True).reshape(-1, size)

    chunk = 8
    block = pl.BlockSpec((1, chunk, points, points), lambda c, part: (c, part, 0, 0))
    halved = jax.ShapeDtypeStruct((3, 2 * clusters * points, 2 * points), BF16)
    whole = pl.BlockSpec(halved.shape, lambda c, part: (0, 0, 0))
    blocks = call(
        blocks_body,
        (halved, halved),
        [SMEM] * 4 + [block] * 2,
        (whole, whole),
        mib=56,
        grid=(clusters, near_max // chunk),
        scratch_shapes=[pltpu.VMEM((6, clusters, 2, points, points), F32)],
    )
    prepare = call(operators_body, jax.ShapeDtypeStruct((kinds // 2, 2 * size, 2 * size), BF16), [VMEM], VMEM)
    sent = call(
        functools.partial(first_moments_body, rows),
        jax.ShapeDtypeStruct((peers * rows, size), F32),
        [VMEM] * 4 + [SMEM] * 2,
        VMEM,
        mib=56,
    )(incident, to_moments, far_source, far_kind, far_count, cluster_box)

    pressure = incident
    for iteration in range(ITERS):
        first, last = iteration == 0, iteration == ITERS - 1
        arrived = exchange(sent, rows if first else 4)
        if first:
            blocks_top, blocks_rest = blocks(near_index, near_count, place, sign, near_real, near_imag)
            operators = prepare(transfer_ops)
        one = lax.ppermute(pressure, "cl", first_swap)
        two = lax.ppermute(pressure, "cl", second_swap)
        piece = jax.ShapeDtypeStruct((peers * 4, size), F32)
        shared = dict(mib=MIB[1], scratch_shapes=[pltpu.VMEM((kinds, 2 * peers, 2 * peers), BF16)])
        if first:
            outs = (piece, jax.ShapeDtypeStruct((peers, size), F32))
            locals_out, lists = call(
                functools.partial(first_transfer_body, rows), outs, [VMEM] * 2, (VMEM, VMEM), **shared
            )(arrived, operators)
        else:
            locals_out = call(next_transfer_body, piece, [VMEM] * 3, VMEM, **shared)(arrived, operators, lists)
        local = exchange(locals_out, 4)
        more = () if first else (incident,)
        base, crossed = call(
            functools.partial(near_body, first), (field, field), [VMEM] * (5 + len(more)), (VMEM, VMEM), mib=MIB[0]
        )(one, pressure, two, blocks_top, blocks_rest, *more)
        crossed = lax.ppermute(crossed, "grp", across)
        pressure, sent = call(
            functools.partial(update_body, last),
            (field, field if last else piece),
            [VMEM] * 3 + [SMEM] + [VMEM] * 3,
            (VMEM, VMEM),
            mib=MIB[2],
        )(local, from_locals, to_moments, cluster_box, base, crossed, pressure)
    return (pressure, sent)


def solution(mesh):
    return jax.shard_map(
        shards,
        mesh=mesh,
        in_specs=(
            P("cl", None, "grp"),
            P("cl", None, None, None),
            P("cl", None, None, None),
            P("cl", None, None),
            P("cl", None, None),
            P(),
            P("cl", None),
            P("cl"),
            P("cl"),
            P("cl", None),
            P("cl", None),
            P("cl"),
        ),
        out_specs=(P("cl", None, "grp"), P("cl", None, "grp")),
        check_vma=False,
    )
```

```python
import functools

import jax
import jax.numpy as jnp
from jax import lax
from jax.experimental import pallas as pl
from jax.experimental.pallas import tpu as pltpu
from jax.sharding import PartitionSpec as P


ITERS = 2
DAMPING = 0.7
MIB = (8, 8, 8)
F32, BF16 = jnp.float32, jnp.bfloat16
VMEM = pl.BlockSpec(memory_space=pltpu.VMEM)
SMEM = pl.BlockSpec(memory_space=pltpu.SMEM)
NT = (((1,), (1,)), ((), ()))
NN = (((1,), (0,)), ((), ()))


def halves(x):
    top = x.astype(BF16)
    return top, (x - top.astype(F32)).astype(BF16)


def dot(a, b, dims=NN):
    return lax.dot_general(a, b, dims, preferred_element_type=F32)


def product(a, b, dims=NN):
    (a0, a1), (b0, b1) = halves(a), halves(b)
    return dot(a0, b0, dims) + (dot(a0, b1, dims) + dot(a1, b0, dims))


def call(body, outs, in_specs, out_specs, mib=8, cycles=0, **more):
    return pl.pallas_call(
        body,
        out_shape=outs,
        in_specs=in_specs,
        out_specs=out_specs,
        compiler_params=pltpu.CompilerParams(vmem_limit_bytes=mib << 20),
        cost_estimate=pl.CostEstimate(flops=cycles, bytes_accessed=1 << 18, transcendentals=0),
        **more,
    )


def send_moments(field, to_moments_ref, box_ref, out_ref, rows):
    count, peers = len(field), out_ref.shape[0] // rows
    series = [product(to_moments_ref[c], field[c]).T for c in range(count)]
    for b in range(count):
        moment = sum(jnp.where(box_ref[c] == b, series[c], 0.0) for c in range(count))
        for k in range(2):
            out_ref[pl.ds(2 * b + k, peers, stride=rows), :] = moment[k * peers : (k + 1) * peers]


def first_moments_body(rows, field_ref, to_moments_ref, source_ref, kind_ref, count_ref, box_ref, out_ref):
    boxes, most = source_ref.shape
    peers = out_ref.shape[0] // rows
    at = lax.broadcasted_iota(jnp.int32, (1, most), 1)
    kinds = [jnp.where(at < count_ref[b], kind_ref[b : b + 1, :], -1) for b in range(boxes)]
    lists = jnp.concatenate([source_ref[b : b + 1, :] for b in range(boxes)] + kinds, axis=1).astype(F32)
    send_moments([field_ref[0], field_ref[1]], to_moments_ref, box_ref, out_ref, rows)
    out_ref[pl.ds(4, peers, stride=rows), :] = jnp.broadcast_to(lists, (peers, lists.shape[1]))
    for row in range(5, rows):
        out_ref[pl.ds(row, peers, stride=rows), :] = jnp.zeros((peers, lists.shape[1]), F32)


def blocks_body(index_ref, count_ref, place_ref, sign_ref, real_ref, imag_ref, top_ref, rest_ref, total):
    odd = lax.rem(place_ref[0], 2)
    c, part = pl.program_id(0), pl.program_id(1)
    chunk = real_ref.shape[1]

    @pl.when((c == 0) & (part == 0))
    def _():
        total[...] = jnp.zeros_like(total)

    for i in range(chunk):
        e = part * chunk + i

        @pl.when(e < count_ref[c])
        def _():
            j = index_ref[c, e]
            total[j, c, 0] += real_ref[0, i]
            total[j, c, 1] += imag_ref[0, i]

    @pl.when((c == pl.num_programs(0) - 1) & (part == pl.num_programs(1) - 1))
    def _():
        points = total.shape[3]
        for j in range(total.shape[0]):
            for cluster in range(total.shape[1]):
                for side in range(2):
                    block = total[j, cluster, side]
                    if side == 1:
                        block = block * sign_ref[0]
                    top, rest = halves(block)
                    row = (cluster * 2 + side) * points
                    slot = (2 - 2 * odd, 1, 2 * odd)[j // 2]
                    here = (slot, pl.ds(row, points), pl.ds(j % 2 * points, points))
                    top_ref[here] = top
                    rest_ref[here] = rest


def operators_body(ops_ref, out_ref):
    size = ops_ref.shape[1]
    for y in range(ops_ref.shape[0]):
        top, rest = halves(ops_ref[y].T)
        rows = pl.ds(y % 2 * size, size)
        out_ref[y // 2, rows, 0:size] = top
        out_ref[y // 2, rows, size : 2 * size] = rest


def near_body(first, first_ref, own_ref, second_ref, top_ref, rest_ref, *rest):
    incident_ref = own_ref if first else rest[0]
    base_ref, crossed_ref = rest[-2:]
    points = own_ref.shape[1]
    total = None
    for slot, ref in enumerate((first_ref, own_ref, second_ref)):
        v0, v1 = halves(jnp.concatenate([ref[0], ref[1]], axis=0))
        both = dot(top_ref[slot], jnp.concatenate([v0, v1], axis=1))
        part = both[:, :points] + (both[:, points:] + dot(rest_ref[slot], v0))
        total = part if total is None else total + part
    for c in range(2):
        base_ref[c] = (incident_ref[c] - own_ref[c]) - total[2 * c * points : (2 * c + 1) * points]
        crossed_ref[c] = total[(2 * c + 1) * points : (2 * c + 2) * points]


def interaction_counts(in_ref, at, rows, counts_ref):
    peers = in_ref.shape[0] // rows
    parts = [in_ref[pl.ds(at + rows * j, peers // 4, stride=4 * rows), :] for j in range(4)]
    lane = lax.broadcasted_iota(jnp.int32, parts[0].shape, 1)
    low = lane < 64
    turn = [pltpu.roll(p, 64, 1) for p in parts]
    source = jnp.concatenate([jnp.where(low, parts[0], turn[1]), jnp.where(low, parts[2], turn[3])], axis=1)
    kind = jnp.concatenate([jnp.where(low, turn[0], parts[1]), jnp.where(low, turn[2], parts[3])], axis=1)
    source, kind = source.astype(jnp.int32), kind.astype(jnp.int32)
    source = (source & 1) * peers + (source >> 1)
    wide = source.shape[1]
    row = lax.broadcasted_iota(jnp.int32, (2 * peers, wide), 0)
    column = lax.broadcasted_iota(jnp.int32, (2 * peers, wide), 1)
    own = (row & 7) == (column >> 5)
    for i in range(peers // 4):
        left = jnp.where(own & ((row >> 3) == kind[i : i + 1, :]), 1.0, 0.0).astype(BF16)
        right = jnp.where(row == source[i : i + 1, :], 1.0, 0.0).astype(BF16)
        block = dot(left, right, NT).astype(BF16)
        for y in range(counts_ref.shape[0]):
            counts_ref[y, 8 * i : 8 * i + 8, :] = block[8 * y : 8 * y + 8]


def transfer(in_ref, ops_ref, counts_ref, out_ref, rows):
    peers, size = in_ref.shape[0] // rows, in_ref.shape[1]
    moments = []
    for k in range(2):
        moments.append(
            jnp.concatenate([in_ref[pl.ds(2 * b + k, peers, stride=rows), :] for b in range(2)], axis=0)
        )
    m0, m1 = halves(jnp.concatenate(moments, axis=1))
    right = jnp.concatenate([m0, m1], axis=0)
    total = [None, None]
    for pair in range(ops_ref.shape[0]):
        grouped = []
        for y in (2 * pair, 2 * pair + 1):
            count = counts_ref[y]
            grouped.append(dot(jnp.concatenate([count, count], axis=1), right))
        for k in range(2):
            g0, g1 = halves(jnp.concatenate([g[:, k * size : (k + 1) * size] for g in grouped], axis=1))
            both = dot(g0, ops_ref[pair])
            part = both[:, :size] + (both[:, size:] + dot(g1, ops_ref[pair, :, :size]))
            total[k] = part if total[k] is None else total[k] + part
    for k in range(2):
        out_ref[pl.ds(k, 2 * peers, stride=2), :] = total[k]


def first_transfer_body(rows, in_ref, ops_ref, out_ref, lists_ref, counts_ref):
    lists_ref[...] = in_ref[pl.ds(4, lists_ref.shape[0], stride=rows), :]
    interaction_counts(in_ref, 4, rows, counts_ref)
    transfer(in_ref, ops_ref, counts_ref, out_ref, rows)


def next_transfer_body(in_ref, ops_ref, lists_ref, out_ref, counts_ref):
    interaction_counts(lists_ref, 0, 1, counts_ref)
    transfer(in_ref, ops_ref, counts_ref, out_ref, 4)


def update_body(last, in_ref, from_locals_ref, box_ref, base_ref, crossed_ref, pressure_ref, *rest):
    peers = in_ref.shape[0] // 4
    local = []
    for b in range(2):
        local.append(jnp.concatenate([in_ref[pl.ds(2 * b + k, peers, stride=4), :] for k in range(2)], axis=0))
    fields = []
    for c in range(2):
        far = product(from_locals_ref[c], jnp.where(box_ref[c] == 0, local[0], local[1]), NT)
        residual = base_ref[c] - (crossed_ref[c] + far)
        field = pressure_ref[c] + DAMPING * residual
        fields.append(field)
        rest[-2][c] = field
        if last:
            rest[-1][c] = residual
    if not last:
        send_moments(fields, rest[0], box_ref, rest[-1], 4)


def shards(
    incident,
    near_real,
    near_imag,
    to_moments,
    from_locals,
    transfer_ops,
    near_index,
    near_count,
    cluster_box,
    far_source,
    far_kind,
    far_count,
):
    clusters, points, _ = incident.shape
    near_max = near_real.shape[1]
    peers, grp = lax.axis_size("cl"), lax.axis_size("grp")
    kinds, size = transfer_ops.shape[0], transfer_ops.shape[1]
    field = jax.ShapeDtypeStruct(incident.shape, F32)
    rows = 5
    first_swap = [(i, i ^ 1) for i in range(peers)]
    second_swap = [(i, (i + 1 if i % 2 else i - 1) % peers) for i in range(peers)]
    across = [(i, (i + grp // 2) % grp) for i in range(grp)]
    sign = jnp.where(lax.axis_index("grp") < grp // 2, 1.0, -1.0).astype(F32).reshape(1)

    place = lax.axis_index("cl").astype(jnp.int32).reshape(1)

    def exchange(x, pieces):
        x = x.reshape((peers, pieces, size) if pieces == 4 else (peers, pieces, 1, size))
        return lax.all_to_all(x, "cl", split_axis=0, concat_axis=0, tiled=True).reshape(-1, size)

    chunk = 8
    block = pl.BlockSpec((1, chunk, points, points), lambda c, part: (c, part, 0, 0))
    halved = jax.ShapeDtypeStruct((3, 2 * clusters * points, 2 * points), BF16)
    whole = pl.BlockSpec(halved.shape, lambda c, part: (0, 0, 0))
    blocks = call(
        blocks_body,
        (halved, halved),
        [SMEM] * 4 + [block] * 2,
        (whole, whole),
        mib=56,
        grid=(clusters, near_max // chunk),
        scratch_shapes=[pltpu.VMEM((6, clusters, 2, points, points), F32)],
    )
    prepare = call(operators_body, jax.ShapeDtypeStruct((kinds // 2, 2 * size, 2 * size), BF16), [VMEM], VMEM)
    sent = call(
        functools.partial(first_moments_body, rows),
        jax.ShapeDtypeStruct((peers * rows, size), F32),
        [VMEM] * 4 + [SMEM] * 2,
        VMEM,
        mib=56,
    )(incident, to_moments, far_source, far_kind, far_count, cluster_box)

    pressure = incident
    for iteration in range(ITERS):
        first, last = iteration == 0, iteration == ITERS - 1
        arrived = exchange(sent, rows if first else 4)
        if first:
            blocks_top, blocks_rest = blocks(near_index, near_count, place, sign, near_real, near_imag)
            operators = prepare(transfer_ops)
        one = lax.ppermute(pressure, "cl", first_swap)
        two = lax.ppermute(pressure, "cl", second_swap)
        piece = jax.ShapeDtypeStruct((peers * 4, size), F32)
        shared = dict(mib=MIB[1], scratch_shapes=[pltpu.VMEM((kinds, 2 * peers, 2 * peers), BF16)])
        if first:
            outs = (piece, jax.ShapeDtypeStruct((peers, size), F32))
            locals_out, lists = call(
                functools.partial(first_transfer_body, rows), outs, [VMEM] * 2, (VMEM, VMEM), **shared
            )(arrived, operators)
        else:
            locals_out = call(next_transfer_body, piece, [VMEM] * 3, VMEM, **shared)(arrived, operators, lists)
        local = exchange(locals_out, 4)
        more = () if first else (incident,)
        base, crossed = call(
            functools.partial(near_body, first), (field, field), [VMEM] * (5 + len(more)), (VMEM, VMEM), mib=MIB[0]
        )(one, pressure, two, blocks_top, blocks_rest, *more)
        crossed = lax.ppermute(crossed, "grp", across)
        pressure, sent = call(
            functools.partial(update_body, last),
            (field, field if last else piece),
            [VMEM] * 2 + [SMEM] + [VMEM] * (3 if last else 4),
            (VMEM, VMEM),
            mib=MIB[2] if last else 57,
        )(local, from_locals, cluster_box, base, crossed, pressure, *(() if last else (to_moments,)))
    return (pressure, sent)


def solution(mesh):
    return jax.shard_map(
        shards,
        mesh=mesh,
        in_specs=(
            P("cl", None, "grp"),
            P("cl", None, None, None),
            P("cl", None, None, None),
            P("cl", None, None),
            P("cl", None, None),
            P(),
            P("cl", None),
            P("cl"),
            P("cl"),
            P("cl", None),
            P("cl", None),
            P("cl"),
        ),
        out_specs=(P("cl", None, "grp"), P("cl", None, "grp")),
        check_vma=False,
    )
```
